32 devices in a mesh: lat: 16 (over z, x, core), chan: 2 (over y).
Axes of the slice: x: 2, y: 2, z: 4, core: 2. Of those that a mesh axis runs over, the one named last changes fastest.
Arguments:
- fields: bfloat16 [6, 96, 192, 768], P(None, 'lat', None, 'chan'), may hold values from -60 to 60, as said below
- kept_lat: int32 [4], replicated, may hold values from 0 to 5, as said below
- kept_lon: int32 [4], replicated, may hold values from 0 to 5, as said below
- spec_w1: bfloat16 [2, 8, 96, 96], P(None, 'chan'), may hold values from -0.4375 to 0.4375
- spec_w2: bfloat16 [2, 8, 96, 96], P(None, 'chan'), may hold values from -0.4375 to 0.4375
- mlp_w1: bfloat16 [768, 3072], replicated, may hold values from -0.21875 to 0.21875
- mlp_w2: bfloat16 [3072, 768], replicated, may hold values from -0.109375 to 0.109375
Outputs:
- block_out: bfloat16 [6, 96, 192, 768], P(None, 'lat', None, 'chan')
The draws below stay inside these ranges and needn't reach their ends.
Inputs may be any that keep to these rules, and one draw needn't show every extreme that they name: `fields`: finite values. `kept_lat`: 4 distinct block numbers in rising order, always holding 0 and 5. `kept_lon`: 4 distinct block numbers in rising order, always holding 0 and 5.
All inputs are finite; a program needn't handle non-finite values.
Results may differ from the reference program's by a relative error of at most 0.0065.
Values may be sent and summed in bfloat16 or wider, within the bound.
No kernel may reach another device: no remote copies, remote signals or barrier semaphores. Data moves between devices by JAX's collectives and lax.ppermute only.
A program may use at most 128 MiB of HBM per device.

```python
import math
import jax
import jax.numpy as jnp
from jax import lax

S = 6
H = 96
W = 192
C = 768
NB = 8
HID = 3072
MB = 16
KBL = 4
KBW = 4
BS = 96
NBL = 6
NBW = 6
KL = 64
KW = 64


def draw_fields(key, part):
    key_base, key_chan, key_token = jax.random.split(key, 3)
    channel_ids = jnp.arange(C, dtype=jnp.float32)
    chan_scale = 10.0 ** (channel_ids / C - 0.5) * jax.random.uniform(key_chan, (C,), jnp.float32, 0.7, 1.4)
    token_scale = 10.0 ** jax.random.uniform(key_token, (S, H, W, 1), jnp.float32, -0.5, 0.5)
    base_draw = jnp.clip(jax.random.normal(key_base, (S, H, W, C), jnp.float32), -4.0, 4.0)
    values = base_draw * token_scale * chan_scale
    return values.astype(jnp.bfloat16)


def pick_blocks(key, block_total, block_count):
    middle_part = jax.random.permutation(key, block_total - 2).astype(jnp.int32) + 1
    chosen = jnp.concatenate([jnp.zeros((1,), jnp.int32), middle_part[:block_count - 2], jnp.full((1,), block_total - 1, jnp.int32)])
    return jnp.sort(chosen)


def draw_kept_lat(key, part):
    return pick_blocks(jax.random.fold_in(key, 11), NBL, KBL)


def draw_kept_lon(key, part):
    return pick_blocks(jax.random.fold_in(key, 23), NBW, KBW)


def level_of(own_key, shape, cuts, smallest, largest):
    gain = 1.0
    for axis_at, blocks in cuts:
        steps = jax.random.uniform(jax.random.fold_in(jax.random.fold_in(own_key, 6), axis_at), (blocks,), jnp.float32, smallest / len(cuts), largest / len(cuts))
        gain = gain * jnp.repeat(jnp.exp(steps), shape[axis_at] // blocks).reshape((-1,) + (1,) * (len(shape) - 1 - axis_at))
    return gain


def noise(rng, shape, deviation, reach, cuts=(), held_as=jnp.bfloat16):
    loudness = level_of(rng, shape, cuts, -0.22, 0.18) if cuts else 1.0
    drawn = jax.random.normal(rng, shape, jnp.float32) * deviation * loudness
    return jnp.minimum(jnp.maximum(drawn, -reach), reach).astype(held_as)


def setup_inputs(seed: int = 0) -> dict:
    arg_keys = jax.random.split(jax.random.key(seed), 8)
    return {
        "fields": draw_fields(jax.random.fold_in(arg_keys[7], 71), 0),
        "kept_lat": draw_kept_lat(jax.random.fold_in(arg_keys[7], 71), 0),
        "kept_lon": draw_kept_lon(jax.random.fold_in(arg_keys[7], 71), 0),
        "spec_w1": noise(arg_keys[3], (2, NB, BS, BS), (2 * BS) ** -0.5, 0.4375, ((1, 2),)),
        "spec_w2": noise(arg_keys[4], (2, NB, BS, BS), (2 * BS) ** -0.5, 0.4375, ((1, 2),)),
        "mlp_w1": noise(arg_keys[5], (C, HID), C ** -0.5, 0.21875),
        "mlp_w2": noise(arg_keys[6], (HID, C), HID ** -0.5, 0.109375),
    }


norm_eps = 1e-05

def mode_list(kept_blocks, block_width):
    offsets = jnp.arange(block_width, dtype=jnp.int32)
    return (kept_blocks.astype(jnp.int32)[:, None] * block_width + offsets[None, :]).reshape(-1)

def lon_forward_table(lon_waves, span_size):
    positions = jnp.arange(span_size, dtype=jnp.int32)
    angle = 2.0 * math.pi / span_size * jnp.mod(positions[:, None] * lon_waves[None, :], span_size).astype(jnp.float32)
    factor = 1.0 / math.sqrt(span_size)
    return jnp.stack([jnp.cos(angle) * factor, -jnp.sin(angle) * factor], axis=1).astype(jnp.bfloat16)

def lon_inverse_table(lon_waves, span_size):
    positions = jnp.arange(span_size, dtype=jnp.int32)
    angle = 2.0 * math.pi / span_size * jnp.mod(lon_waves[:, None] * positions[None, :], span_size).astype(jnp.float32)
    factor = jnp.where(lon_waves > 0, 2.0, 1.0).astype(jnp.float32)[:, None] / math.sqrt(span_size)
    return jnp.stack([jnp.cos(angle) * factor, -jnp.sin(angle) * factor], axis=1).astype(jnp.bfloat16)

def lat_forward_table(lat_waves, row_ids, height):
    angle = 2.0 * math.pi / height * jnp.mod(lat_waves[:, None] * row_ids[None, :], height).astype(jnp.float32)
    cosine = jnp.cos(angle) / math.sqrt(height)
    sine = jnp.sin(angle) / math.sqrt(height)
    upper = jnp.stack([cosine, sine], axis=-1)
    lower = jnp.stack([-sine, cosine], axis=-1)
    return jnp.stack([upper, lower], axis=1).astype(jnp.bfloat16)

def lat_inverse_table(row_ids, lat_waves, height):
    angle = 2.0 * math.pi / height * jnp.mod(row_ids[:, None] * lat_waves[None, :], height).astype(jnp.float32)
    cosine = jnp.cos(angle) / math.sqrt(height)
    sine = jnp.sin(angle) / math.sqrt(height)
    upper = jnp.stack([cosine, -sine], axis=-1)
    lower = jnp.stack([sine, cosine], axis=-1)
    return jnp.stack([upper, lower], axis=1).astype(jnp.bfloat16)

def complex_weight(weights):
    real_part = weights[0]
    imag_part = weights[1]
    return jnp.stack([jnp.stack([real_part, imag_part], axis=2), jnp.stack([-imag_part, real_part], axis=2)], axis=0)

def spectral_filter(modes, weight_one, weight_two):
    layer_one = jnp.einsum('kmsni,snioj->kmonj', modes.astype(jnp.float32), complex_weight(weight_one).astype(jnp.float32))
    layer_one = jnp.maximum(layer_one, 0.0).astype(jnp.bfloat16)
    layer_two = jnp.einsum('kmsni,snioj->kmonj', layer_one.astype(jnp.float32), complex_weight(weight_two).astype(jnp.float32))
    return layer_two.astype(jnp.bfloat16)

def layer_norm(values):
    average = lax.optimization_barrier(jnp.mean(values, axis=-1, keepdims=True))
    spread = lax.optimization_barrier(jnp.mean(values * values, axis=-1, keepdims=True)) - average * average
    return (values - average) * lax.rsqrt(spread + norm_eps)

def reference(fields, kept_lat, kept_lon, spec_w1, spec_w2, mlp_w1, mlp_w2):
    lat_waves = mode_list(kept_lat, MB)
    lon_waves = mode_list(kept_lon, MB)
    row_ids = jnp.arange(H, dtype=jnp.int32)
    forward_lon = lon_forward_table(lon_waves, W).astype(jnp.float32)
    inverse_lon = lon_inverse_table(lon_waves, W).astype(jnp.float32)
    forward_lat = lat_forward_table(lat_waves, row_ids, H).astype(jnp.float32)
    inverse_lat = lat_inverse_table(row_ids, lat_waves, H).astype(jnp.float32)

    def section_one(block_rows):
        normed = layer_norm(block_rows.astype(jnp.float32)).astype(jnp.bfloat16)
        return jnp.einsum('hwc,wsm->hmsc', normed.astype(jnp.float32), forward_lon).astype(jnp.bfloat16)

    def section_two(inputs_pair):
        block_rows, wave_rows = inputs_pair
        field_values = block_rows.astype(jnp.float32)
        normed = layer_norm(field_values).astype(jnp.bfloat16)
        spectral = jnp.einsum('hmsc,msw->hwc', wave_rows.astype(jnp.float32), inverse_lon)
        mixed = (field_values + normed.astype(jnp.float32) + spectral).astype(jnp.bfloat16)
        normed_two = layer_norm(mixed.astype(jnp.float32)).astype(jnp.bfloat16)
        hidden = jax.nn.gelu(jnp.dot(normed_two.reshape(-1, C), mlp_w1, preferred_element_type=jnp.float32), approximate=False).astype(jnp.bfloat16)
        result = mixed.astype(jnp.float32).reshape(-1, C) + jnp.dot(hidden, mlp_w2, preferred_element_type=jnp.float32)
        return result.astype(jnp.bfloat16).reshape(8, W, C)

    def one_sample(sample_fields):
        row_blocks = sample_fields.reshape(H // 8, 8, W, C)
        along = lax.map(section_one, row_blocks).reshape(H, KW, 2, C)
        spectrum = jnp.einsum('kohs,hmsc->kmoc', forward_lat, along.astype(jnp.float32)).astype(jnp.bfloat16)
        filtered = spectral_filter(spectrum.reshape(KL, KW, 2, NB, BS), spec_w1, spec_w2).reshape(KL, KW, 2, C)
        wave = jnp.einsum('hoks,kmsc->hmoc', inverse_lat, filtered.astype(jnp.float32)).astype(jnp.bfloat16)
        block_out = lax.map(section_two, (row_blocks, wave.reshape(H // 8, 8, KW, 2, C)))
        return block_out.reshape(H, W, C)
    return lax.map(one_sample, fields)
```

```python
import math

import jax
import jax.numpy as jnp
from jax import lax
from jax.experimental import pallas as pl
from jax.experimental.pallas import tpu as pltpu
from jax.sharding import PartitionSpec as P

MB = 16


norm_eps = 1e-05


def mode_list(kept_blocks, block_width):
    offsets = jnp.arange(block_width, dtype=jnp.int32)
    return (kept_blocks[:, None] * block_width + offsets[None, :]).reshape(-1)


def lon_forward_table(lon_waves, span_size):
    positions = jnp.arange(span_size, dtype=jnp.int32)
    angle = (
        2.0
        * math.pi
        / span_size
        * jnp.mod(positions[:, None] * lon_waves[None, :], span_size).astype(jnp.float32)
    )
    factor = 1.0 / math.sqrt(span_size)
    return jnp.stack([jnp.cos(angle) * factor, -jnp.sin(angle) * factor], axis=1).astype(
        jnp.bfloat16
    )


def lon_inverse_table(lon_waves, span_size):
    positions = jnp.arange(span_size, dtype=jnp.int32)
    angle = (
        2.0
        * math.pi
        / span_size
        * jnp.mod(lon_waves[:, None] * positions[None, :], span_size).astype(jnp.float32)
    )
    factor = jnp.where(lon_waves > 0, 2.0, 1.0).astype(jnp.float32)[:, None] / math.sqrt(span_size)
    return jnp.stack([jnp.cos(angle) * factor, -jnp.sin(angle) * factor], axis=1).astype(
        jnp.bfloat16
    )


def lat_forward_table(lat_waves, row_ids, height):
    angle = (
        2.0
        * math.pi
        / height
        * jnp.mod(lat_waves[:, None] * row_ids[None, :], height).astype(jnp.float32)
    )
    cosine = jnp.cos(angle) / math.sqrt(height)
    sine = jnp.sin(angle) / math.sqrt(height)
    upper = jnp.stack([cosine, sine], axis=-1)
    lower = jnp.stack([-sine, cosine], axis=-1)
    return jnp.stack([upper, lower], axis=1).astype(jnp.bfloat16)


def lat_inverse_table(row_ids, lat_waves, height):
    angle = (
        2.0
        * math.pi
        / height
        * jnp.mod(row_ids[:, None] * lat_waves[None, :], height).astype(jnp.float32)
    )
    cosine = jnp.cos(angle) / math.sqrt(height)
    sine = jnp.sin(angle) / math.sqrt(height)
    upper = jnp.stack([cosine, -sine], axis=-1)
    lower = jnp.stack([sine, cosine], axis=-1)
    return jnp.stack([upper, lower], axis=1).astype(jnp.bfloat16)


def complex_weight(weights):
    real_part = weights[0]
    imag_part = weights[1]
    return jnp.stack(
        [jnp.stack([real_part, imag_part], axis=2), jnp.stack([-imag_part, real_part], axis=2)],
        axis=0,
    )


def spectral_filter(modes, weight_one, weight_two):
    layer_one = jnp.einsum(
        "kmsni,snioj->kmonj", modes, complex_weight(weight_one), preferred_element_type=jnp.float32
    )
    layer_one = jnp.maximum(layer_one, 0.0).astype(jnp.bfloat16)
    layer_two = jnp.einsum(
        "kmsni,snioj->kmonj",
        layer_one,
        complex_weight(weight_two),
        preferred_element_type=jnp.float32,
    )
    return layer_two.astype(jnp.bfloat16)


def layer_norm(values):
    average = jnp.mean(values, axis=-1, keepdims=True)
    spread = jnp.mean(values * values, axis=-1, keepdims=True) - average * average
    return (values - average) * lax.rsqrt(spread + norm_eps)


def on_device_general(fields, kept_lat, kept_lon, spec_w1, spec_w2, mlp_w1, mlp_w2):
    samples, rows_here, span_size, chans = fields.shape
    lat_count = lax.axis_size("lat")
    chan_count = lax.axis_size("chan")
    total_chans = chans * chan_count
    height = rows_here * lat_count
    blocks_here = spec_w1.shape[1]
    block_size = spec_w1.shape[2]
    lat_waves = mode_list(kept_lat, MB)
    lon_waves = mode_list(kept_lon, MB)
    lat_modes = lat_waves.shape[0]
    lon_modes = lon_waves.shape[0]
    field_values = fields.astype(jnp.float32)
    moments = lax.psum(
        (jnp.sum(field_values, axis=3), jnp.sum(field_values * field_values, axis=3)), "chan"
    )
    average = moments[0] / total_chans
    spread = moments[1] / total_chans - average * average
    normed = ((field_values - average[..., None]) * lax.rsqrt(spread[..., None] + norm_eps)).astype(
        jnp.bfloat16
    )
    along = jnp.einsum(
        "nhwc,wsm->nhmsc",
        normed,
        lon_forward_table(lon_waves, span_size),
        preferred_element_type=jnp.float32,
    )
    along = along.astype(jnp.bfloat16).reshape(samples, rows_here, lon_modes, 2 * chans)
    all_rows = jnp.arange(height, dtype=jnp.int32)
    columns = lax.all_to_all(along, "lat", split_axis=2, concat_axis=1, tiled=True)
    col_modes = columns.shape[2]
    spectrum = jnp.einsum(
        "kohs,nhmsc->nkmoc",
        lat_forward_table(lat_waves, all_rows, height),
        columns.reshape(samples, height, col_modes, 2, chans),
        preferred_element_type=jnp.float32,
    ).astype(jnp.bfloat16)
    filtered = spectral_filter(
        spectrum.reshape(samples * lat_modes, col_modes, 2, blocks_here, block_size),
        spec_w1,
        spec_w2,
    )
    wave_cols = jnp.einsum(
        "hoks,nkmsc->nhmoc",
        lat_inverse_table(all_rows, lat_waves, height),
        filtered.reshape(samples, lat_modes, col_modes, 2, chans),
        preferred_element_type=jnp.float32,
    ).astype(jnp.bfloat16)
    wave = lax.all_to_all(
        wave_cols.reshape(samples, height, col_modes, 2 * chans),
        "lat",
        split_axis=1,
        concat_axis=2,
        tiled=True,
    ).reshape(samples, rows_here, lon_modes, 2, chans)
    spectral = jnp.einsum(
        "nhmsc,msw->nhwc",
        wave,
        lon_inverse_table(lon_waves, span_size),
        preferred_element_type=jnp.float32,
    )
    mixed = (field_values + normed.astype(jnp.float32) + spectral).astype(jnp.bfloat16)
    cell_values = lax.all_to_all(mixed, "chan", split_axis=2, concat_axis=3, tiled=True).astype(
        jnp.float32
    )
    normed_two = layer_norm(cell_values).astype(jnp.bfloat16)
    hidden = jax.nn.gelu(
        jnp.einsum("nkwc,cf->nkwf", normed_two, mlp_w1, preferred_element_type=jnp.float32),
        approximate=False,
    ).astype(jnp.bfloat16)
    result = (
        cell_values
        + jnp.einsum("nkwf,fc->nkwc", hidden, mlp_w2, preferred_element_type=jnp.float32)
    ).astype(jnp.bfloat16)
    return lax.all_to_all(result, "chan", split_axis=3, concat_axis=2, tiled=True)


LANES = 128
PACK = 16
CHUNK = 1
HIDDEN_STEP = 512


def longitude_kernel(normed_ref, table_ref, out_ref):
    _, pair, span, chans = normed_ref.shape
    cells = normed_ref[0].reshape(pair * span, chans)
    modes = jnp.dot(table_ref[...], cells, preferred_element_type=jnp.float32).astype(jnp.bfloat16)
    for tile in range(chans // LANES):
        piece = modes[:, tile * LANES : (tile + 1) * LANES]
        out_ref[:, 0, 0, tile] = piece.reshape(out_ref.shape[0], PACK, LANES)


def spectrum_kernel(cols_ref, forward_ref, one_ref, two_ref, inverse_ref, out_ref):
    tiles = cols_ref.shape[3]
    rows = forward_ref.shape[1]
    half = forward_ref.shape[0] // 2
    chans = tiles * LANES
    cols = jnp.concatenate([cols_ref[:, 0, :, t].reshape(rows, LANES) for t in range(tiles)], axis=1)
    spectrum = jnp.dot(forward_ref[...], cols, preferred_element_type=jnp.float32)
    spectrum = spectrum.astype(jnp.bfloat16)
    modes = jnp.concatenate([spectrum[:half], spectrum[half:]], axis=1)
    hidden = jnp.dot(modes, one_ref[...], preferred_element_type=jnp.float32)
    hidden = jnp.maximum(hidden, 0.0).astype(jnp.bfloat16)
    filtered = jnp.dot(hidden, two_ref[...], preferred_element_type=jnp.float32)
    filtered = filtered.astype(jnp.bfloat16)
    stacked = jnp.concatenate([filtered[:, :chans], filtered[:, chans:]], axis=0)
    wave = jnp.dot(inverse_ref[...], stacked, preferred_element_type=jnp.float32)
    wave = wave.astype(jnp.bfloat16)
    for tile in range(tiles):
        piece = wave[:, tile * LANES : (tile + 1) * LANES]
        out_ref[:, 0, :, tile] = piece.reshape(
            out_ref.shape[0], out_ref.shape[2], PACK, LANES
        )


def mix_kernel(place_ref, wave_ref, table_ref, fields_ref, normed_ref, own_ref, peer_ref):
    tiles = wave_ref.shape[3]
    rows = table_ref.shape[1]
    pair, part, chans = own_ref.shape[1:]
    waves = jnp.concatenate([wave_ref[:, 0, 0, t].reshape(rows, LANES) for t in range(tiles)], axis=1)
    spectral = jnp.dot(table_ref[...], waves, preferred_element_type=jnp.float32)
    place = place_ref[0]
    for half, out_ref in enumerate((own_ref, peer_ref)):
        start = pl.multiple_of((place if half == 0 else 1 - place) * part, part)
        for row in range(pair):
            at = (half * pair + row) * part
            total = fields_ref[0, row, pl.ds(start, part)].astype(jnp.float32)
            total = total + normed_ref[0, row, pl.ds(start, part)].astype(jnp.float32)
            out_ref[0, row] = (total + spectral[at : at + part]).astype(jnp.bfloat16)


def exact_gelu(values):
    return values * (1.0 + lax.erf(values * math.sqrt(0.5))) * 0.5


def mlp_kernel(
    place_ref,
    own_ref,
    peer_ref,
    one_own_ref,
    one_peer_ref,
    two_own_ref,
    two_peer_ref,
    out_own_ref,
    out_peer_ref,
    norm_own_ref,
    norm_peer_ref,
    sum_own_ref,
    sum_peer_ref,
):
    step = pl.program_id(1)
    tokens, chans = norm_own_ref.shape

    @pl.when(step == 0)
    def _():
        own = own_ref[0].reshape(tokens, chans).astype(jnp.float32)
        peer = peer_ref[0].reshape(tokens, chans).astype(jnp.float32)
        total = 2 * chans
        average = jnp.sum(own + peer, axis=1, keepdims=True) / total
        square = jnp.sum(own * own + peer * peer, axis=1, keepdims=True) / total
        scale = lax.rsqrt(square - average * average + norm_eps)
        norm_own_ref[...] = ((own - average) * scale).astype(jnp.bfloat16)
        norm_peer_ref[...] = ((peer - average) * scale).astype(jnp.bfloat16)
        sum_own_ref[...] = own
        sum_peer_ref[...] = peer

    hidden = jnp.dot(norm_own_ref[...], one_own_ref[...], preferred_element_type=jnp.float32)
    hidden = hidden + jnp.dot(norm_peer_ref[...], one_peer_ref[...], preferred_element_type=jnp.float32)
    hidden = exact_gelu(hidden).astype(jnp.bfloat16)
    sum_own_ref[...] += jnp.dot(hidden, two_own_ref[...], preferred_element_type=jnp.float32)
    sum_peer_ref[...] += jnp.dot(hidden, two_peer_ref[...], preferred_element_type=jnp.float32)

    @pl.when(step == pl.num_programs(1) - 1)
    def _():
        out_own_ref[0] = sum_own_ref[...].astype(jnp.bfloat16).reshape(out_own_ref.shape[1:])
        out_peer_ref[0] = sum_peer_ref[...].astype(jnp.bfloat16).reshape(out_peer_ref.shape[1:])


def paired_weight(weights):
    blocks, size = weights.shape[1:3]
    eye = jnp.eye(blocks, dtype=weights.dtype)
    dense = weights[:, :, :, None, :] * eye[None, :, None, :, None]
    dense = dense.reshape(2, blocks * size, blocks * size)
    upper = jnp.concatenate([dense[0], dense[1]], axis=1)
    lower = jnp.concatenate([-dense[1], dense[0]], axis=1)
    return jnp.concatenate([upper, lower], axis=0)


def fits(rows_here, chans, chan_count, lon_here, span_size):
    return (
        chan_count == 2
        and 2 * lon_here <= PACK
        and PACK % (2 * lon_here) == 0
        and rows_here % (PACK // (2 * lon_here)) == 0
        and chans % LANES == 0
        and (span_size // chan_count) % PACK == 0
    )


def on_device(fields, kept_lat, kept_lon, spec_w1, spec_w2, mlp_w1, mlp_w2):
    samples, rows_here, span_size, chans = fields.shape
    lat_count = lax.axis_size("lat")
    chan_count = lax.axis_size("chan")
    lon_here = kept_lon.shape[0] * MB // lat_count
    if not fits(rows_here, chans, chan_count, lon_here, span_size):
        return on_device_general(fields, kept_lat, kept_lon, spec_w1, spec_w2, mlp_w1, mlp_w2)
    total_chans = chans * chan_count
    height = rows_here * lat_count
    lat_waves = mode_list(kept_lat, MB)
    lon_waves = mode_list(kept_lon, MB)
    lat_modes = lat_waves.shape[0]
    pair = PACK // (2 * lon_here)
    pairs = rows_here // pair
    tiles = chans // LANES
    part = span_size // chan_count
    place = lax.axis_index("chan").astype(jnp.int32)
    swap = [(0, 1), (1, 0)]
    eye_pair = jnp.eye(pair, dtype=jnp.bfloat16)
    eye_lon = jnp.eye(lon_here, dtype=jnp.bfloat16)

    lon_table = lon_forward_table(lon_waves, span_size).transpose(2, 1, 0)
    lon_table = lon_table.reshape(lat_count, 1, lon_here, 2, 1, span_size)
    lon_table = (lon_table * eye_pair[None, :, None, None, :, None]).reshape(
        lat_count * PACK, pair * span_size
    )
    all_rows = jnp.arange(height, dtype=jnp.int32)
    lat_table = lat_forward_table(lat_waves, all_rows, height).transpose(1, 0, 2, 3)
    lat_table = lat_table[:, None, :, :, None, :] * eye_lon[None, :, None, None, :, None]
    lat_table = lat_table.reshape(2 * lon_here * lat_modes, height * lon_here * 2)
    lat_back = lat_inverse_table(all_rows, lat_waves, height).transpose(0, 1, 3, 2)
    lat_back = lat_back[:, None, :, :, None, :] * eye_lon[None, :, None, None, :, None]
    lat_back = lat_back.reshape(height * lon_here * 2, 2 * lon_here * lat_modes)
    lon_back = lon_inverse_table(lon_waves, span_size)
    lon_back = lon_back.reshape(lat_count, lon_here, 2, chan_count, part)
    lon_back = jnp.where(place == 0, lon_back, lon_back[:, :, :, ::-1])
    lon_back = lon_back.transpose(3, 4, 0, 1, 2)[:, None, :, :, None]
    lon_back = lon_back * eye_pair[None, :, None, None, :, None, None]
    lon_back = lon_back.reshape(chan_count * pair * part, lat_count * PACK)
    weight_one = paired_weight(spec_w1)
    weight_two = paired_weight(spec_w2)
    places = place.reshape(1)

    field_values = fields.astype(jnp.float32)
    moments = jnp.stack(
        [jnp.sum(field_values, axis=3), jnp.sum(field_values * field_values, axis=3)]
    )
    moments = moments + lax.ppermute(moments, "chan", swap)
    average = moments[0] / total_chans
    spread = moments[1] / total_chans - average * average
    normed = ((field_values - average[..., None]) * lax.rsqrt(spread[..., None] + norm_eps)).astype(
        jnp.bfloat16
    )

    count = CHUNK
    sent_shape = (lat_count, count, pairs, tiles, PACK, LANES)
    half_shape = (count, rows_here, part, chans)
    steps = mlp_w1.shape[1] // HIDDEN_STEP
    tokens = rows_here * part

    def longitude(first):
        return pl.pallas_call(
            longitude_kernel,
            grid=(count, pairs),
            in_specs=[
                pl.BlockSpec((1, pair, span_size, chans), lambda n, p: (first + n, p, 0, 0)),
                pl.BlockSpec(lon_table.shape, lambda n, p: (0, 0)),
            ],
            out_specs=pl.BlockSpec(
                (lat_count, 1, 1, tiles, PACK, LANES), lambda n, p: (0, n, p, 0, 0, 0)
            ),
            out_shape=jax.ShapeDtypeStruct(sent_shape, jnp.bfloat16),
            name="longitude",
        )(normed, lon_table)

    def spectrum(cols):
        block = (lat_count, 1, pairs, tiles, PACK, LANES)
        return pl.pallas_call(
            spectrum_kernel,
            grid=(count,),
            in_specs=[
                pl.BlockSpec(block, lambda n: (0, n, 0, 0, 0, 0)),
                pl.BlockSpec(lat_table.shape, lambda n: (0, 0)),
                pl.BlockSpec(weight_one.shape, lambda n: (0, 0)),
                pl.BlockSpec(weight_two.shape, lambda n: (0, 0)),
                pl.BlockSpec(lat_back.shape, lambda n: (0, 0)),
            ],
            out_specs=pl.BlockSpec(block, lambda n: (0, n, 0, 0, 0, 0)),
            out_shape=jax.ShapeDtypeStruct(sent_shape, jnp.bfloat16),
            name="spectrum",
        )(cols, lat_table, weight_one, weight_two, lat_back)

    def mix(wave, first):
        half = pl.BlockSpec((1, pair, part, chans), lambda n, p, at: (n, p, 0, 0))
        whole = pl.BlockSpec((1, pair, span_size, chans), lambda n, p, at: (first + n, p, 0, 0))
        return pl.pallas_call(
            mix_kernel,
            grid_spec=pltpu.PrefetchScalarGridSpec(
                num_scalar_prefetch=1,
                grid=(count, pairs),
                in_specs=[
                    pl.BlockSpec(
                        (lat_count, 1, 1, tiles, PACK, LANES), lambda n, p, at: (0, n, p, 0, 0, 0)
                    ),
                    pl.BlockSpec(lon_back.shape, lambda n, p, at: (0, 0)),
                    whole,
                    whole,
                ],
                out_specs=[half, half],
            ),
            out_shape=[jax.ShapeDtypeStruct(half_shape, jnp.bfloat16)] * 2,
            name="mix",
        )(places, wave, lon_back, fields, normed)

    def mlp(own, peer):
        half = pl.BlockSpec((1, rows_here, part, chans), lambda n, f, at: (n, 0, 0, 0))
        return pl.pallas_call(
            mlp_kernel,
            grid_spec=pltpu.PrefetchScalarGridSpec(
                num_scalar_prefetch=1,
                grid=(count, steps),
                in_specs=[
                    half,
                    half,
                    pl.BlockSpec((chans, HIDDEN_STEP), lambda n, f, at: (at[0], f)),
                    pl.BlockSpec((chans, HIDDEN_STEP), lambda n, f, at: (1 - at[0], f)),
                    pl.BlockSpec((HIDDEN_STEP, chans), lambda n, f, at: (f, at[0])),
                    pl.BlockSpec((HIDDEN_STEP, chans), lambda n, f, at: (f, 1 - at[0])),
                ],
                out_specs=[half, half],
                scratch_shapes=[
                    pltpu.VMEM((tokens, chans), jnp.bfloat16),
                    pltpu.VMEM((tokens, chans), jnp.bfloat16),
                    pltpu.VMEM((tokens, chans), jnp.float32),
                    pltpu.VMEM((tokens, chans), jnp.float32),
                ],
            ),
            out_shape=[jax.ShapeDtypeStruct(half_shape, jnp.bfloat16)] * 2,
            name="mlp",
        )(places, own, peer, mlp_w1, mlp_w1, mlp_w2, mlp_w2)

    def exchange(values):
        return lax.all_to_all(values, "lat", split_axis=0, concat_axis=0, tiled=True)

    results = []
    for first in range(0, samples, count):
        cols = exchange(longitude(first))
        wave = exchange(spectrum(cols))
        own, peer = mix(wave, first)
        peer = lax.ppermute(peer, "chan", swap)
        own, peer = mlp(own, peer)
        peer = lax.ppermute(peer, "chan", swap)
        results.append(
            jnp.where(
                place == 0,
                jnp.concatenate([own, peer], axis=2),
                jnp.concatenate([peer, own], axis=2),
            )
        )
    return jnp.concatenate(results, axis=0)


def solution(mesh):
    placed = (
        P(None, "lat", None, "chan"),
        P(),
        P(),
        P(None, "chan", None, None),
        P(None, "chan", None, None),
        P(),
        P(),
    )
    return jax.shard_map(
        on_device,
        mesh=mesh,
        in_specs=placed,
        out_specs=P(None, "lat", None, "chan"),
        check_vma=False,
    )
```
